256 devices in a mesh: row: 16 (over z_hi, y), col: 16 (over z_lo, x, core).
Axes of the slice: x: 4, y: 4, z: 8 (z_hi: 4, z_lo: 2; z = z_hi * 2 + z_lo), core: 2. Of those that a mesh axis runs over, the one named last changes fastest.
Arguments:
- spectra: bfloat16 [4096, 128], P(('row', 'col')), may hold values from -6 to 6
- residual: bfloat16 [768, 128, 128, 128], P(('row', 'col')), may hold values from -1.5 to 1.5
- slot_tile: int32 [768], P(('row', 'col')), may hold values from -1 to 527, as said below
- tile_blocks: int32 [528, 2], replicated, may hold values from 0 to 31, as said below
Outputs:
- spectra_grad: float32 [4096, 128], P(('row', 'col'))
The draws below stay inside these ranges and needn't reach their ends.
Inputs may be any that keep to these rules, and one draw needn't show every extreme that they name: `slot_tile`: every tile number appears in exactly one slot and all other slots hold -1. A tile with row block p and column block q sits on the device at mesh position (p mod 16, q mod 16), that is device number (p mod 16) * 16 + q mod 16 in the order of row+col. `tile_blocks`: row t holds the row block and the column block of tile t, the row block no larger than the column block; every such pair of blocks is exactly one tile.
All inputs are finite; a program needn't handle non-finite values.
Results may differ from the reference program's by a relative error of at most 0.004.
Values may be sent and summed in bfloat16 or wider, within the bound.
No kernel may reach another device: no remote copies, remote signals or barrier semaphores. Data moves between devices by JAX's collectives and lax.ppermute only.
A program may use at most 128 MiB of HBM per device.

```python
import math
import jax
import jax.numpy as jnp
import numpy as np
from jax import lax

F = 64
L = 128
BS = 128
SLOTS = 3
NB = 32
S = 4096
NT = 528
SLOT_ROWS = 768
N_ROW = 16
N_COL = 16
DEVICES = 256


def tile_layout(key):
    base = jax.random.fold_in(key, 7)
    key_perm, key_rank, key_shift = jax.random.split(base, 3)
    upper_rows, upper_cols = np.triu_indices(NB)
    canon_rows = jnp.asarray(upper_rows.astype(np.int32))
    canon_cols = jnp.asarray(upper_cols.astype(np.int32))
    numbering = jax.random.permutation(key_perm, NT).astype(jnp.int32)
    canon_pairs = jnp.stack([canon_rows, canon_cols], axis=1)
    tile_table = jnp.zeros((NT, 2), jnp.int32).at[numbering].set(canon_pairs)
    device_of = canon_rows % N_ROW * N_COL + canon_cols % N_COL
    rank_keys = jax.random.permutation(key_rank, NT).astype(jnp.int32)
    same_device = device_of[:, None] == device_of[None, :]
    earlier = rank_keys[None, :] < rank_keys[:, None]
    ranks = jnp.sum((same_device & earlier).astype(jnp.int32), axis=1)
    shifts = jax.random.randint(key_shift, (DEVICES,), 0, SLOTS).astype(jnp.int32)
    slot_of = (ranks + shifts[device_of]) % SLOTS
    slot_table = jnp.full((DEVICES * SLOTS,), -1, jnp.int32).at[device_of * SLOTS + slot_of].set(numbering)
    return (slot_table, tile_table)


def draw_slot_tile(key, part):
    slot_table, tile_table = tile_layout(key)
    return slot_table


def draw_tile_blocks(key, part):
    slot_table, tile_table = tile_layout(key)
    return tile_table


def steps_of(own_key, extent, pieces, least, high):
    def one(dim, shards_of):
        heights = jax.random.uniform(jax.random.fold_in(jax.random.fold_in(own_key, 6), dim), (shards_of,), jnp.float32, least / len(pieces), high / len(pieces))
        return jnp.repeat(jnp.exp(heights), extent[dim] // shards_of).reshape((-1,) + (1,) * (len(extent) - dim - 1))

    loudness = one(*pieces[0])
    for cut in pieces[1:]:
        loudness = loudness * one(*cut)
    return loudness


def scatter_about(stream_key, shape, scale, most, pieces=(), kind=jnp.bfloat16):
    result = jax.random.normal(stream_key, shape, jnp.float32) * scale
    if len(pieces) > 0:
        result = steps_of(stream_key, shape, pieces, -0.22, 0.18) * result
    return jnp.clip(result, min=-most, max=most).astype(kind)


def setup_inputs(seed: int = 0) -> dict:
    key_of = jax.random.split(jax.random.key(seed), 5)
    spectra = scatter_about(key_of[0], (S, 2 * F), 1.0, 6.0, ((0, 256),))
    residual = scatter_about(key_of[1], (SLOT_ROWS, BS, BS, L), 0.25, 1.5, ((0, 256),))
    slot_tile = draw_slot_tile(jax.random.fold_in(key_of[4], 71), 0)
    tile_blocks = draw_tile_blocks(jax.random.fold_in(key_of[4], 71), 0)
    return dict(spectra=spectra, residual=residual, slot_tile=slot_tile, tile_blocks=tile_blocks)


def dft_table(lag_count, freq_count):
    lag_index = jnp.arange(lag_count, dtype=jnp.int32) - lag_count // 2
    freq_index = jnp.arange(freq_count, dtype=jnp.int32)
    phase_steps = (lag_index[:, None] * freq_index[None, :]) % lag_count
    angles = phase_steps.astype(jnp.float32) * (2.0 * math.pi / lag_count)
    cosine = jnp.cos(angles) / lag_count
    sine = -jnp.sin(angles) / lag_count
    return jnp.concatenate([cosine, sine], axis=1).astype(jnp.bfloat16)


def pair_terms(spectral, row_spec, col_spec, freq_count):
    real_part = spectral[:, :, :freq_count]
    imag_part = spectral[:, :, freq_count:]
    row_re = row_spec[:, :freq_count].astype(jnp.float32)
    row_im = row_spec[:, freq_count:].astype(jnp.float32)
    col_re = col_spec[:, :freq_count].astype(jnp.float32)
    col_im = col_spec[:, freq_count:].astype(jnp.float32)
    row_gain_re = jnp.sum(real_part * col_re[None] - imag_part * col_im[None], axis=1)
    row_gain_im = jnp.sum(real_part * col_im[None] + imag_part * col_re[None], axis=1)
    col_gain_re = jnp.sum(real_part * row_re[:, None] + imag_part * row_im[:, None], axis=0)
    col_gain_im = jnp.sum(real_part * row_im[:, None] - imag_part * row_re[:, None], axis=0)
    row_gain = jnp.concatenate([row_gain_re, row_gain_im], axis=1)
    col_gain = jnp.concatenate([col_gain_re, col_gain_im], axis=1)
    return row_gain, col_gain


def block_major(flat):
    per_row = NB // N_ROW
    piece = BS // N_COL
    grid = flat.reshape(N_ROW, N_COL, per_row, piece, flat.shape[1])
    return jnp.transpose(grid, (2, 0, 1, 3, 4)).reshape(NB, BS, flat.shape[1])


def station_major(blocks):
    per_row = NB // N_ROW
    piece = BS // N_COL
    grid = blocks.reshape(per_row, N_ROW, N_COL, piece, blocks.shape[2])
    return jnp.transpose(grid, (1, 2, 0, 3, 4)).reshape(S, blocks.shape[2])


def add_block(gradient, contrib, index):
    current = lax.dynamic_index_in_dim(gradient, index, 0, keepdims=True)
    return lax.dynamic_update_index_in_dim(gradient, current + contrib[None], index, 0)


def reference(spectra, residual, slot_tile, tile_blocks):
    dft = dft_table(L, F)
    station_ids = jnp.arange(BS, dtype=jnp.int32)
    upper = station_ids[:, None] < station_ids[None, :]
    block_spec = block_major(spectra)

    def one_slot(gradient, slot_index):
        tile_id = slot_tile[slot_index]
        filled = tile_id >= 0
        safe_id = jnp.maximum(tile_id, 0)
        row_block = tile_blocks[safe_id, 0].astype(jnp.int32)
        col_block = tile_blocks[safe_id, 1].astype(jnp.int32)
        pair_mask = (jnp.where(row_block == col_block, upper, True) & filled).astype(jnp.float32)
        tile_data = lax.dynamic_index_in_dim(residual, slot_index, 0, keepdims=False)
        spectral = jnp.dot(tile_data.reshape(BS * BS, L), dft, preferred_element_type=jnp.float32)
        spectral = spectral.reshape(BS, BS, 2 * F) * pair_mask[:, :, None]
        row_spec = lax.dynamic_index_in_dim(block_spec, row_block, 0, keepdims=False)
        col_spec = lax.dynamic_index_in_dim(block_spec, col_block, 0, keepdims=False)
        row_gain, col_gain = pair_terms(spectral, row_spec, col_spec, F)
        gradient = add_block(gradient, row_gain, row_block)
        gradient = add_block(gradient, col_gain, col_block)
        return gradient, None

    start_grad = jnp.zeros((NB, BS, 2 * F), jnp.float32)
    gradient, _ = lax.scan(one_slot, start_grad, jnp.arange(SLOT_ROWS, dtype=jnp.int32))
    return station_major(gradient)
```

```python
import functools
import math

import jax
import jax.numpy as jnp
import ml_dtypes
import numpy as np
from jax import lax
from jax.experimental import pallas as pl
from jax.experimental.pallas import tpu as pltpu
from jax.sharding import PartitionSpec as P

F = 64
L = 128
BS = 128
SLOTS = 3
NB = 32
CHUNK = 64
N_CHUNK = BS // CHUNK
UNROLL = 16


def dft_pair():
    lag = np.arange(L, dtype=np.int64) - L // 2
    freq = np.arange(F, dtype=np.int64)
    steps = (lag[:, None] * freq[None, :]) % L
    angles = steps.astype(np.float32) * np.float32(2.0 * math.pi / L)
    table = np.concatenate([np.cos(angles) / L, -np.sin(angles) / L], axis=1)
    zero = np.zeros((L, 2 * F))
    return np.block([[table, zero], [zero, table]]).astype(ml_dtypes.bfloat16)


def spec_pair(spec_ref, upper, filled):
    both = spec_ref[...].astype(jnp.float32)
    block = jnp.where(upper == 1, both[:, BS // 16 :, :], both[:, : BS // 16, :])
    block = block.reshape(BS, 2 * F) * filled
    return block, pltpu.roll(block, F, axis=1)


def load_all(res_hbm, buf, sems):
    for s in range(SLOTS):
        for c in range(N_CHUNK):
            pltpu.make_async_copy(
                res_hbm.at[s, pl.ds(c * CHUNK, CHUNK)],
                buf.at[s, pl.ds(c * CHUNK, CHUNK)],
                sems.at[s, c],
            ).start()


def wait_chunk(res_hbm, buf, sems, s, c):
    pltpu.make_async_copy(
        res_hbm.at[s, pl.ds(c * CHUNK, CHUNK)], buf.at[s, pl.ds(c * CHUNK, CHUNK)], sems.at[s, c]
    ).wait()


def mask_chunk(buf, s, first):
    def one(n, carry):
        i = first + n
        rows = lax.broadcasted_iota(jnp.int32, (BS, L), 0)
        keep = jnp.where(rows > i, 1.0, 0.0).astype(jnp.bfloat16)
        buf[s, i] = buf[s, i] * keep
        return carry

    lax.fori_loop(0, CHUNK, one, 0)


def decode(enc_ref, s):
    code = enc_ref[s]
    filled = jnp.where(code > 0, 1.0, 0.0).astype(jnp.float32)
    tile = jnp.maximum(code - 1, 0)
    p = tile // NB
    q = tile - p * NB
    return p, q, filled


def col_kernel(enc_ref, spec_ref, dft_ref, res_hbm, out_ref, buf, one_ref, two_ref, acc_ref, sems):
    load_all(res_hbm, buf, sems)
    acc_ref[...] = jnp.zeros_like(acc_ref)

    def slot(s, carry):
        p, q, filled = decode(enc_ref, s)
        one, two = spec_pair(spec_ref, p // 16, filled)
        one_ref[...] = one
        two_ref[...] = two
        total = (jnp.zeros((BS, 2 * F), jnp.float32),) * 2
        for c in range(N_CHUNK):
            wait_chunk(res_hbm, buf, sems, s, c)

            @pl.when(p == q)
            def _():
                mask_chunk(buf, s, c * CHUNK)

            def step(n, total):
                t1, t2 = total
                base = c * CHUNK + n * UNROLL
                for u in range(0, UNROLL, 2):
                    lhs = jnp.concatenate([buf[s, base + u], buf[s, base + u + 1]], axis=1)
                    g = jnp.dot(lhs, dft_ref[...], preferred_element_type=jnp.float32)
                    for h in range(2):
                        gh = g[:, h * L : (h + 1) * L]
                        t1 = t1 + gh * one_ref[pl.ds(base + u + h, 1), :]
                        t2 = t2 + gh * two_ref[pl.ds(base + u + h, 1), :]
                return t1, t2

            total = lax.fori_loop(0, CHUNK // UNROLL, step, total)
        t1, t2 = total
        lane = lax.broadcasted_iota(jnp.int32, (BS, 2 * F), 1)
        gain = jnp.where(lane < F, t1 + pltpu.roll(t1, F, axis=1), pltpu.roll(t2, F, axis=1) - t2)
        gain = gain.reshape(16, BS // 16, 2 * F)
        for h in range(2):
            rows = pl.ds(h * 8, 8)

            @pl.when(q // 16 == h)
            def _():
                acc_ref[:, rows, :] = acc_ref[:, rows, :] + gain

        return carry

    lax.fori_loop(0, SLOTS, slot, 0)
    out_ref[...] = acc_ref[...].astype(out_ref.dtype)


def row_kernel(enc_ref, spec_ref, dft_ref, res_hbm, out_ref, buf, one_ref, two_ref, part1, part2, sems):
    load_all(res_hbm, buf, sems)
    out_ref[...] = jnp.zeros_like(out_ref)

    def slot(s, carry):
        p, q, filled = decode(enc_ref, s)
        one, two = spec_pair(spec_ref, q // 16, filled)
        one_ref[...] = one
        two_ref[...] = two
        for c in range(N_CHUNK):
            wait_chunk(res_hbm, buf, sems, s, c)

            @pl.when(p == q)
            def _():
                mask_chunk(buf, s, c * CHUNK)

            def step(n, carry):
                base = c * CHUNK + n * UNROLL
                for u in range(0, UNROLL, 2):
                    lhs = jnp.concatenate([buf[s, base + u], buf[s, base + u + 1]], axis=1)
                    g = jnp.dot(lhs, dft_ref[...], preferred_element_type=jnp.float32)
                    for h in range(2):
                        gh = g[:, h * L : (h + 1) * L]
                        for ref, part in ((one_ref, part1), (two_ref, part2)):
                            prod = (gh * ref[...]).reshape(BS // 8, 8, 2 * F)
                            at = pl.multiple_of((base + u + h) * 8, 8)
                            part[pl.ds(at, 8), :] = jnp.sum(prod, axis=0)
                return carry

            lax.fori_loop(0, CHUNK // UNROLL, step, 0)
        t1 = jnp.zeros((BS, 2 * F), jnp.float32)
        t2 = jnp.zeros((BS, 2 * F), jnp.float32)
        for k in range(8):
            t1 = t1 + part1[pl.ds(k, BS, stride=8), :]
            t2 = t2 + part2[pl.ds(k, BS, stride=8), :]
        lane = lax.broadcasted_iota(jnp.int32, (BS, 2 * F), 1)
        gain = jnp.where(lane < F, t1 - pltpu.roll(t1, F, axis=1), pltpu.roll(t2, F, axis=1) + t2)
        gain = gain.reshape(16, BS // 16, 2 * F)
        for h in range(2):
            rows = pl.ds(h * 8, 8)

            @pl.when(p // 16 == h)
            def _():
                out_ref[:, rows, :] = out_ref[:, rows, :] + gain

        return carry

    lax.fori_loop(0, SLOTS, slot, 0)


def call(kernel, name, out_dtype, scratch, enc, spec, dft, residual):
    vmem = pl.BlockSpec(memory_space=pltpu.VMEM)
    return pl.pallas_call(
        kernel,
        name=name,
        out_shape=jax.ShapeDtypeStruct((16, 16, 2 * F), out_dtype),
        in_specs=[
            pl.BlockSpec(memory_space=pltpu.SMEM),
            vmem,
            vmem,
            pl.BlockSpec(memory_space=pl.ANY),
        ],
        out_specs=vmem,
        scratch_shapes=[
            pltpu.VMEM((SLOTS, BS, BS, L), jnp.bfloat16),
            pltpu.VMEM((BS, 2 * F), jnp.float32),
            pltpu.VMEM((BS, 2 * F), jnp.float32),
            *scratch,
            pltpu.SemaphoreType.DMA((SLOTS, N_CHUNK)),
        ],
        compiler_params=pltpu.CompilerParams(vmem_limit_bytes=24 << 20),
        cost_estimate=pl.CostEstimate(
            flops=SLOTS * BS * BS * L * 2 * F * 2, bytes_accessed=residual.size * 2, transcendentals=0
        ),
    )(enc, spec, dft, residual)


def on_device(spectra, residual, slot_tile, tile_blocks):
    tiles = jnp.arange(tile_blocks.shape[0], dtype=jnp.int32)
    code = tile_blocks[:, 0] * NB + tile_blocks[:, 1] + 1
    enc = jnp.sum(jnp.where(slot_tile[:, None] == tiles[None, :], code[None, :], 0), axis=1)
    dft = jnp.asarray(dft_pair())
    swap = [(a * 16 + b, b * 16 + a) for a in range(16) for b in range(16)]
    spread = jnp.broadcast_to(spectra[None], (16, 16, 2 * F))
    row_spec = lax.all_to_all(spread, "col", 0, 0)
    col_spec = lax.ppermute(row_spec, ("row", "col"), swap)
    acc = pltpu.VMEM((16, 16, 2 * F), jnp.float32)
    part = pltpu.VMEM((BS * 8, 2 * F), jnp.float32)
    col_gain = call(col_kernel, "col_gain", jnp.bfloat16, [acc], enc, row_spec, dft, residual)
    moved = lax.ppermute(col_gain, ("row", "col"), swap)
    row_gain = call(row_kernel, "row_gain", jnp.float32, [part, part], enc, col_spec, dft, residual)
    total = (row_gain + moved.astype(jnp.float32)).astype(jnp.bfloat16)
    pieces = lax.all_to_all(total, "col", 0, 0)
    return jnp.sum(pieces.astype(jnp.float32), axis=0)


def solution(mesh):
    return jax.shard_map(
        on_device,
        mesh=mesh,
        in_specs=(
            P(("row", "col"), None),
            P(("row", "col"), None, None, None),
            P(("row", "col")),
            P(),
        ),
        out_specs=P(("row", "col"), None),
        check_vma=False,
    )
```

```python
import functools
import math

import jax
import jax.numpy as jnp
import ml_dtypes
import numpy as np
from jax import lax
from jax.experimental import pallas as pl
from jax.experimental.pallas import tpu as pltpu
from jax.sharding import PartitionSpec as P

F = 64
L = 128
BS = 128
SLOTS = 3
NB = 32
CHUNK = 64
PARTS = SLOTS * BS // CHUNK
PER = BS // CHUNK
ROW_UNROLL = 16
VMEM_COL = 12 << 20
VMEM_ROW = 8 << 20


def dft_pair():
    lag = np.arange(L, dtype=np.int64) - L // 2
    freq = np.arange(F, dtype=np.int64)
    steps = (lag[:, None] * freq[None, :]) % L
    angles = steps.astype(np.float32) * np.float32(2.0 * math.pi / L)
    table = np.concatenate([np.cos(angles) / L, -np.sin(angles) / L], axis=1)
    zero = np.zeros((L, 2 * F))
    return np.block([[table, zero], [zero, table]]).astype(ml_dtypes.bfloat16)


def spec_pair(spec_ref, upper, filled):
    both = spec_ref[...].astype(jnp.float32)
    block = jnp.where(upper == 1, both[:, BS // 16 :, :], both[:, : BS // 16, :])
    block = block.reshape(BS, 2 * F) * filled.astype(jnp.float32)
    return block, pltpu.roll(block, F, axis=1)


def add_gain(ref, gain, half):
    gain = gain.reshape(16, BS // 16, 2 * F)
    for h in range(2):
        rows = pl.ds(h * 8, 8)

        @pl.when(half == h)
        def _():
            ref[:, rows, :] = ref[:, rows, :] + gain


def chunk_copy(res_hbm, buf, sems, h, slot):
    return pltpu.make_async_copy(res_hbm.at[pl.ds(h * CHUNK, CHUNK)], buf.at[slot], sems.at[slot])


def mask_chunk(buf, slot, first):
    def one(n, carry):
        rows = lax.broadcasted_iota(jnp.int32, (BS, L), 0)
        keep = jnp.where(rows > first + n, 1.0, 0.0).astype(jnp.bfloat16)
        buf[slot, n] = buf[slot, n] * keep
        return carry

    lax.fori_loop(0, CHUNK, one, 0)


def col_kernel(
    slot_hbm, table_hbm, dft_hbm, res_hbm, spec_ref, out_ref, g_ref, meta_ref,
    buf, dft_ref, slot_ref, table_ref, one_ref, two_ref, acc_ref, sems,
):
    small = [
        pltpu.make_async_copy(src, dst, sems.at[2 + n])
        for n, (src, dst) in enumerate(((slot_hbm, slot_ref), (table_hbm, table_ref), (dft_hbm, dft_ref)))
    ]
    for copy in small:
        copy.start()
    chunk_copy(res_hbm, buf, sems, 0, 0).start()
    acc_ref[...] = jnp.zeros_like(acc_ref)
    for copy in small:
        copy.wait()
    for s in range(SLOTS):
        tile = slot_ref[s]
        safe = jnp.maximum(tile, 0)
        meta_ref[s] = table_ref[0, safe]
        meta_ref[SLOTS + s] = table_ref[1, safe]
        meta_ref[2 * SLOTS + s] = jnp.where(tile >= 0, 1, 0)

    def part(h, carry):
        s = h // PER
        first = (h - s * PER) * CHUNK
        slot = lax.rem(h, 2)
        p, q, filled = meta_ref[s], meta_ref[SLOTS + s], meta_ref[2 * SLOTS + s]

        @pl.when(h + 1 < PARTS)
        def _():
            chunk_copy(res_hbm, buf, sems, h + 1, 1 - slot).start()

        one, two = spec_pair(spec_ref, p // 16, filled)
        one_ref[...] = one
        two_ref[...] = two
        chunk_copy(res_hbm, buf, sems, h, slot).wait()

        @pl.when(p == q)
        def _():
            mask_chunk(buf, slot, first)

        t1 = jnp.zeros((BS, 2 * F), jnp.float32)
        t2 = jnp.zeros((BS, 2 * F), jnp.float32)
        for u in range(0, CHUNK, 2):
            lhs = jnp.concatenate([buf[slot, u], buf[slot, u + 1]], axis=1)
            g = jnp.dot(lhs, dft_ref[...], preferred_element_type=jnp.float32)
            for k in range(2):
                gk = g[:, k * L : (k + 1) * L]
                g_ref[h * CHUNK + u + k] = gk
                t1 = t1 + gk * one_ref[pl.ds(first + u + k, 1), :]
                t2 = t2 + gk * two_ref[pl.ds(first + u + k, 1), :]
        lane = lax.broadcasted_iota(jnp.int32, (BS, 2 * F), 1)
        gain = jnp.where(lane < F, t1 + pltpu.roll(t1, F, axis=1), pltpu.roll(t2, F, axis=1) - t2)
        add_gain(acc_ref, gain, q // 16)
        return carry

    lax.fori_loop(0, PARTS, part, 0)
    out_ref[...] = acc_ref[...].astype(out_ref.dtype)


def row_kernel(meta_ref, spec_ref, g_ref, out_ref, one_ref, two_ref, part1, part2):
    out_ref[...] = jnp.zeros_like(out_ref)

    def slot(s, carry):
        p, q, filled = meta_ref[s], meta_ref[SLOTS + s], meta_ref[2 * SLOTS + s]
        one, two = spec_pair(spec_ref, q // 16, filled)
        one_ref[...] = one
        two_ref[...] = two

        def step(n, carry):
            for u in range(ROW_UNROLL):
                i = n * ROW_UNROLL + u
                g = g_ref[s * BS + i]
                at = pl.multiple_of(i * 8, 8)
                for ref, part in ((one_ref, part1), (two_ref, part2)):
                    prod = (g * ref[...]).reshape(BS // 8, 8, 2 * F)
                    part[pl.ds(at, 8), :] = jnp.sum(prod, axis=0)
            return carry

        lax.fori_loop(0, BS // ROW_UNROLL, step, 0)
        t1 = jnp.zeros((BS, 2 * F), jnp.float32)
        t2 = jnp.zeros((BS, 2 * F), jnp.float32)
        for k in range(8):
            t1 = t1 + part1[pl.ds(k, BS, stride=8), :]
            t2 = t2 + part2[pl.ds(k, BS, stride=8), :]
        lane = lax.broadcasted_iota(jnp.int32, (BS, 2 * F), 1)
        gain = jnp.where(lane < F, t1 - pltpu.roll(t1, F, axis=1), pltpu.roll(t2, F, axis=1) + t2)
        add_gain(out_ref, gain, p // 16)
        return carry

    lax.fori_loop(0, SLOTS, slot, 0)


def f32(*shape):
    return pltpu.VMEM(shape, jnp.float32)


VM = pl.BlockSpec(memory_space=pltpu.VMEM)
SM = pl.BlockSpec(memory_space=pltpu.SMEM)


def cost(flops, moved):
    return pl.CostEstimate(flops=flops, bytes_accessed=moved, transcendentals=0)


def gain_col(slot_tile, table, dft, residual, spec):
    far = pl.BlockSpec(memory_space=pl.ANY)
    held = [pltpu.with_memory_space_constraint(x, pltpu.HBM) for x in (slot_tile, table, dft, residual)]
    return pl.pallas_call(
        col_kernel,
        name="col_gain",
        out_shape=(
            jax.ShapeDtypeStruct((16, 16, 2 * F), jnp.bfloat16),
            jax.ShapeDtypeStruct((SLOTS * BS, BS, 2 * F), jnp.float32),
            jax.ShapeDtypeStruct((3 * SLOTS,), jnp.int32),
        ),
        in_specs=[far, far, far, far, VM],
        out_specs=(VM, VM, SM),
        scratch_shapes=[
            pltpu.VMEM((2, CHUNK, BS, L), jnp.bfloat16),
            pltpu.VMEM((2 * L, 4 * F), jnp.bfloat16),
            pltpu.SMEM((SLOTS,), jnp.int32),
            pltpu.SMEM(table.shape, jnp.int32),
            f32(BS, 2 * F),
            f32(BS, 2 * F),
            f32(16, 16, 2 * F),
            pltpu.SemaphoreType.DMA((5,)),
        ],
        compiler_params=pltpu.CompilerParams(vmem_limit_bytes=VMEM_COL),
        cost_estimate=cost(SLOTS * BS * BS * L * 2 * F * 4, residual.size * 2),
    )(*held, spec)


def gain_row(meta, spec, g):
    return pl.pallas_call(
        row_kernel,
        name="row_gain",
        out_shape=jax.ShapeDtypeStruct((16, 16, 2 * F), jnp.float32),
        in_specs=[SM, VM, VM],
        out_specs=VM,
        scratch_shapes=[f32(BS, 2 * F), f32(BS, 2 * F), f32(BS * 8, 2 * F), f32(BS * 8, 2 * F)],
        compiler_params=pltpu.CompilerParams(vmem_limit_bytes=VMEM_ROW),
        cost_estimate=cost(g.size * 4, g.size * 4),
    )(meta, spec, g)


def hops(a, b, k):
    def ring(u, v, n):
        return min((u - v) % n, (v - u) % n)

    z = ring(a // 4 * 2 + b // 8, b // 4 * 2 + k // 8, 8)
    return z + ring(a % 4, b % 4, 4) + ring(b // 2 % 4, k // 2 % 4, 4)


def assign(cost):
    n = len(cost)
    u, v, row, way = [0] * (n + 1), [0] * (n + 1), [0] * (n + 1), [0] * (n + 1)
    for i in range(1, n + 1):
        row[0], at = i, 0
        least, used = [math.inf] * (n + 1), [False] * (n + 1)
        while row[at]:
            used[at] = True
            delta, nxt = math.inf, 0
            for j in range(1, n + 1):
                if not used[j]:
                    c = cost[row[at] - 1][j - 1] - u[row[at]] - v[j]
                    if c < least[j]:
                        least[j], way[j] = c, at
                    if least[j] < delta:
                        delta, nxt = least[j], j
            for j in range(n + 1):
                if used[j]:
                    u[row[j]] += delta
                    v[j] -= delta
                else:
                    least[j] -= delta
            at = nxt
        while at:
            row[at] = row[way[at]]
            at = way[at]
    return {row[j] - 1: j - 1 for j in range(1, n + 1)}


def partners():
    pairs = []
    for b in range(16):
        chosen = assign([[6 ** hops(a, b, k) for k in range(16)] for a in range(16)])
        pairs += [(a * 16 + b, b * 16 + chosen[a]) for a in range(16)]
    return pairs


def on_device(spectra, residual, slot_tile, tile_blocks):
    table = tile_blocks.T
    dft = jnp.asarray(dft_pair())
    pairs = partners()
    spread = jnp.broadcast_to(spectra[None], (16, 16, 2 * F))
    row_spec = lax.all_to_all(spread, "col", 0, 0)
    col_spec = lax.ppermute(row_spec, ("row", "col"), [(v, u) for u, v in pairs])
    col_gain, g, meta = gain_col(slot_tile, table, dft, residual.reshape(SLOTS * BS, BS, L), row_spec)
    moved = lax.ppermute(col_gain, ("row", "col"), pairs)
    row_gain = gain_row(meta, col_spec, g)
    total = (row_gain + moved.astype(jnp.float32)).astype(jnp.bfloat16)
    pieces = lax.all_to_all(total, "col", 0, 0)
    return jnp.sum(pieces.astype(jnp.float32), axis=0)


def solution(mesh):
    return jax.shard_map(
        on_device,
        mesh=mesh,
        in_specs=(
            P(("row", "col"), None),
            P(("row", "col"), None, None, None),
            P(("row", "col")),
            P(),
        ),
        out_specs=P(("row", "col"), None),
        check_vma=False,
    )
```

```python
import functools
import math

import jax
import jax.numpy as jnp
import ml_dtypes
import numpy as np
from jax import lax
from jax.experimental import pallas as pl
from jax.experimental.pallas import tpu as pltpu
from jax.sharding import PartitionSpec as P

F = 64
L = 128
BS = 128
SLOTS = 3
NB = 32
CHUNK = 128
PARTS = SLOTS * BS // CHUNK
PER = BS // CHUNK
ROW_UNROLL = 32
VMEM_COL = 11 << 20
VMEM_ROW = 8 << 20


def dft_pair():
    lag = np.arange(L, dtype=np.int64) - L // 2
    freq = np.arange(F, dtype=np.int64)
    steps = (lag[:, None] * freq[None, :]) % L
    angles = steps.astype(np.float32) * np.float32(2.0 * math.pi / L)
    table = np.concatenate([np.cos(angles) / L, -np.sin(angles) / L], axis=1)
    zero = np.zeros((L, 2 * F))
    return np.block([[table, zero], [zero, table]]).astype(ml_dtypes.bfloat16)


def spec_pair(spec_ref, upper, filled):
    both = spec_ref[...].astype(jnp.float32)
    block = jnp.where(upper == 1, both[:, BS // 16 :, :], both[:, : BS // 16, :])
    block = block.reshape(BS, 2 * F) * filled.astype(jnp.float32)
    return block, pltpu.roll(block, F, axis=1)


def add_gain(ref, gain, half):
    gain = gain.reshape(16, BS // 16, 2 * F)
    for h in range(2):
        rows = pl.ds(h * 8, 8)

        @pl.when(half == h)
        def _():
            ref[:, rows, :] = ref[:, rows, :] + gain


def chunk_copy(res_hbm, buf, sems, h, slot):
    return pltpu.make_async_copy(res_hbm.at[pl.ds(h * CHUNK, CHUNK)], buf.at[slot], sems.at[slot])


def mask_chunk(buf, slot, first):
    tile = 16

    def one(r, carry):
        rows = lax.broadcasted_iota(jnp.int32, (tile, L), 0)
        keep = jnp.where(rows > r, 1.0, 0.0).astype(jnp.bfloat16)
        for m in range(CHUNK // tile):
            below = first + m * tile
            at = m * tile + r
            if below:
                buf[slot, at, :below, :] = jnp.zeros((below, L), jnp.bfloat16)
            own = slice(below, below + tile)
            buf[slot, at, own, :] = buf[slot, at, own, :] * keep
        return carry

    lax.fori_loop(0, tile, one, 0)


def col_kernel(
    slot_hbm, table_hbm, dft_hbm, res_hbm, spec_ref, out_ref, g_ref, meta_ref,
    buf, dft_ref, slot_ref, table_ref, one_ref, two_ref, acc_ref, sems,
):
    small = [
        pltpu.make_async_copy(src, dst, sems.at[2 + n])
        for n, (src, dst) in enumerate(((slot_hbm, slot_ref), (table_hbm, table_ref), (dft_hbm, dft_ref)))
    ]
    for copy in small:
        copy.start()
    chunk_copy(res_hbm, buf, sems, 0, 0).start()
    acc_ref[...] = jnp.zeros_like(acc_ref)
    for copy in small:
        copy.wait()
    for s in range(SLOTS):
        tile = slot_ref[s]
        safe = jnp.maximum(tile, 0)
        meta_ref[s] = table_ref[0, safe]
        meta_ref[SLOTS + s] = table_ref[1, safe]
        meta_ref[2 * SLOTS + s] = jnp.where(tile >= 0, 1, 0)

    for s in range(SLOTS):
        one, two = spec_pair(spec_ref, meta_ref[s] // 16, meta_ref[2 * SLOTS + s])
        one_ref[s * BS : (s + 1) * BS, :] = one
        two_ref[s * BS : (s + 1) * BS, :] = two

    def part(h, carry):
        s = h // PER
        first = (h - s * PER) * CHUNK
        slot = lax.rem(h, 2)
        p, q = meta_ref[s], meta_ref[SLOTS + s]

        @pl.when(h + 1 < PARTS)
        def _():
            chunk_copy(res_hbm, buf, sems, h + 1, 1 - slot).start()

        chunk_copy(res_hbm, buf, sems, h, slot).wait()

        for c in range(PER):

            @pl.when((p == q) & (first == c * CHUNK))
            def _():
                mask_chunk(buf, slot, c * CHUNK)

        half = q // 16
        t1 = jnp.zeros((BS, 2 * F), jnp.float32)
        t2 = jnp.zeros((BS, 2 * F), jnp.float32)
        for u in range(0, CHUNK, 2):
            lhs = jnp.concatenate([buf[slot, u], buf[slot, u + 1]], axis=1)
            g = jnp.dot(lhs, dft_ref[...], preferred_element_type=jnp.float32)
            for k in range(2):
                gk = g[:, k * L : (k + 1) * L]
                g_ref[h * CHUNK + u + k] = gk
                t1 = t1 + gk * one_ref[pl.ds(h * CHUNK + u + k, 1), :]
                t2 = t2 + gk * two_ref[pl.ds(h * CHUNK + u + k, 1), :]
        acc_ref[half, 0] += t1
        acc_ref[half, 1] += t2
        return carry

    lax.fori_loop(0, PARTS, part, 0)
    lane = lax.broadcasted_iota(jnp.int32, (BS, 2 * F), 1)
    for half in range(2):
        t1, t2 = acc_ref[half, 0], acc_ref[half, 1]
        gain = jnp.where(lane < F, t1 + pltpu.roll(t1, F, axis=1), pltpu.roll(t2, F, axis=1) - t2)
        out_ref[:, half * 8 : (half + 1) * 8, :] = gain.reshape(16, BS // 16, 2 * F).astype(out_ref.dtype)


def row_kernel(meta_ref, spec_ref, g_ref, out_ref, one_ref, two_ref, part1, part2):
    out_ref[...] = jnp.zeros_like(out_ref)

    def slot(s, carry):
        p, q, filled = meta_ref[s], meta_ref[SLOTS + s], meta_ref[2 * SLOTS + s]
        one, two = spec_pair(spec_ref, q // 16, filled)
        one_ref[...] = one
        two_ref[...] = two

        def step(n, carry):
            for u in range(ROW_UNROLL):
                i = n * ROW_UNROLL + u
                g = g_ref[s * BS + i]
                at = pl.multiple_of(i * 8, 8)
                for ref, part in ((one_ref, part1), (two_ref, part2)):
                    prod = (g * ref[...]).reshape(BS // 8, 8, 2 * F)
                    part[pl.ds(at, 8), :] = jnp.sum(prod, axis=0)
            return carry

        lax.fori_loop(0, BS // ROW_UNROLL, step, 0)
        t1 = jnp.zeros((BS, 2 * F), jnp.float32)
        t2 = jnp.zeros((BS, 2 * F), jnp.float32)
        for k in range(8):
            t1 = t1 + part1[pl.ds(k, BS, stride=8), :]
            t2 = t2 + part2[pl.ds(k, BS, stride=8), :]
        lane = lax.broadcasted_iota(jnp.int32, (BS, 2 * F), 1)
        gain = jnp.where(lane < F, t1 - pltpu.roll(t1, F, axis=1), pltpu.roll(t2, F, axis=1) + t2)
        add_gain(out_ref, gain, p // 16)
        return carry

    lax.fori_loop(0, SLOTS, slot, 0)


def f32(*shape):
    return pltpu.VMEM(shape, jnp.float32)


VM = pl.BlockSpec(memory_space=pltpu.VMEM)
SM = pl.BlockSpec(memory_space=pltpu.SMEM)


def cost(flops, moved):
    return pl.CostEstimate(flops=flops, bytes_accessed=moved, transcendentals=0)


def gain_col(slot_tile, table, dft, residual, spec):
    far = pl.BlockSpec(memory_space=pl.ANY)
    held = [pltpu.with_memory_space_constraint(x, pltpu.HBM) for x in (slot_tile, table, dft, residual)]
    return pl.pallas_call(
        col_kernel,
        name="col_gain",
        out_shape=(
            jax.ShapeDtypeStruct((16, 16, 2 * F), jnp.bfloat16),
            jax.ShapeDtypeStruct((SLOTS * BS, BS, 2 * F), jnp.float32),
            jax.ShapeDtypeStruct((3 * SLOTS,), jnp.int32),
        ),
        in_specs=[far, far, far, far, VM],
        out_specs=(VM, VM, SM),
        scratch_shapes=[
            pltpu.VMEM((2, CHUNK, BS, L), jnp.bfloat16),
            pltpu.VMEM((2 * L, 4 * F), jnp.bfloat16),
            pltpu.SMEM((SLOTS,), jnp.int32),
            pltpu.SMEM(table.shape, jnp.int32),
            f32(SLOTS * BS, 2 * F),
            f32(SLOTS * BS, 2 * F),
            f32(2, 2, BS, 2 * F),
            pltpu.SemaphoreType.DMA((5,)),
        ],
        compiler_params=pltpu.CompilerParams(vmem_limit_bytes=VMEM_COL),
        cost_estimate=cost(SLOTS * BS * BS * L * 2 * F * 4, residual.size * 2),
    )(*held, spec)


def gain_row(meta, spec, g):
    return pl.pallas_call(
        row_kernel,
        name="row_gain",
        out_shape=jax.ShapeDtypeStruct((16, 16, 2 * F), jnp.float32),
        in_specs=[SM, VM, VM],
        out_specs=VM,
        scratch_shapes=[f32(BS, 2 * F), f32(BS, 2 * F), f32(BS * 8, 2 * F), f32(BS * 8, 2 * F)],
        compiler_params=pltpu.CompilerParams(vmem_limit_bytes=VMEM_ROW),
        cost_estimate=cost(g.size * 4, g.size * 4),
    )(meta, spec, g)


def hops(a, b, k):
    def ring(u, v, n):
        return min((u - v) % n, (v - u) % n)

    z = ring(a // 4 * 2 + b // 8, b // 4 * 2 + k // 8, 8)
    return z + ring(a % 4, b % 4, 4) + ring(b // 2 % 4, k // 2 % 4, 4)


def assign(cost):
    n = len(cost)
    u, v, row, way = [0] * (n + 1), [0] * (n + 1), [0] * (n + 1), [0] * (n + 1)
    for i in range(1, n + 1):
        row[0], at = i, 0
        least, used = [math.inf] * (n + 1), [False] * (n + 1)
        while row[at]:
            used[at] = True
            delta, nxt = math.inf, 0
            for j in range(1, n + 1):
                if not used[j]:
                    c = cost[row[at] - 1][j - 1] - u[row[at]] - v[j]
                    if c < least[j]:
                        least[j], way[j] = c, at
                    if least[j] < delta:
                        delta, nxt = least[j], j
            for j in range(n + 1):
                if used[j]:
                    u[row[j]] += delta
                    v[j] -= delta
                else:
                    least[j] -= delta
            at = nxt
        while at:
            row[at] = row[way[at]]
            at = way[at]
    return {row[j] - 1: j - 1 for j in range(1, n + 1)}


def partners():
    pairs = []
    for b in range(16):
        chosen = assign([[6 ** hops(a, b, k) for k in range(16)] for a in range(16)])
        pairs += [(a * 16 + b, b * 16 + chosen[a]) for a in range(16)]
    return pairs


def on_device(spectra, residual, slot_tile, tile_blocks):
    table = tile_blocks.T
    dft = jnp.asarray(dft_pair())
    pairs = partners()
    spread = jnp.broadcast_to(spectra[None], (16, 16, 2 * F))
    row_spec = lax.all_to_all(spread, "col", 0, 0)
    col_spec = lax.ppermute(row_spec, ("row", "col"), [(v, u) for u, v in pairs])
    col_gain, g, meta = gain_col(slot_tile, table, dft, residual.reshape(SLOTS * BS, BS, L), row_spec)
    moved = lax.ppermute(col_gain, ("row", "col"), pairs)
    row_gain = gain_row(meta, col_spec, g)
    total = (row_gain + moved.astype(jnp.float32)).astype(jnp.bfloat16)
    pieces = lax.all_to_all(total, "col", 0, 0)
    return jnp.sum(pieces.astype(jnp.float32), axis=0)


def solution(mesh):
    return jax.shard_map(
        on_device,
        mesh=mesh,
        in_specs=(
            P(("row", "col"), None),
            P(("row", "col"), None, None, None),
            P(("row", "col")),
            P(),
        ),
        out_specs=P(("row", "col"), None),
        check_vma=False,
    )
```

```python
import functools
import math

import jax
import jax.numpy as jnp
import ml_dtypes
import numpy as np
from jax import lax
from jax.experimental import pallas as pl
from jax.experimental.pallas import tpu as pltpu
from jax.sharding import PartitionSpec as P

F = 64
L = 128
BS = 128
SLOTS = 3
NB = 32
CHUNK = 128
PARTS = SLOTS * BS // CHUNK
PER = BS // CHUNK
ROW_UNROLL = 32
VMEM_COL = 14 << 20
VMEM_ROW = 8 << 20


def dft_pair():
    lag = np.arange(L, dtype=np.int64) - L // 2
    freq = np.arange(F, dtype=np.int64)
    steps = (lag[:, None] * freq[None, :]) % L
    angles = steps.astype(np.float32) * np.float32(2.0 * math.pi / L)
    table = np.concatenate([np.cos(angles) / L, -np.sin(angles) / L], axis=1)
    zero = np.zeros((L, 2 * F))
    return np.block([[table, zero], [zero, table]]).astype(ml_dtypes.bfloat16)


def spec_pair(spec_ref, upper, filled):
    both = spec_ref[...].astype(jnp.float32)
    block = jnp.where(upper == 1, both[:, BS // 16 :, :], both[:, : BS // 16, :])
    block = block.reshape(BS, 2 * F) * filled.astype(jnp.float32)
    return block, pltpu.roll(block, F, axis=1)


def add_gain(ref, gain, half):
    gain = gain.reshape(16, BS // 16, 2 * F)
    for h in range(2):
        rows = pl.ds(h * 8, 8)

        @pl.when(half == h)
        def _():
            ref[:, rows, :] = ref[:, rows, :] + gain


def chunk_copy(res_hbm, buf, sems, h, slot):
    return pltpu.make_async_copy(res_hbm.at[pl.ds(h * CHUNK, CHUNK)], buf.at[slot], sems.at[slot])


def mask_chunk(buf, slot, first):
    tile = 16

    def one(r, carry):
        rows = lax.broadcasted_iota(jnp.int32, (tile, L), 0)
        keep = jnp.where(rows > r, 1.0, 0.0).astype(jnp.bfloat16)
        for m in range(CHUNK // tile):
            below = first + m * tile
            at = m * tile + r
            if below:
                buf[slot, at, :below, :] = jnp.zeros((below, L), jnp.bfloat16)
            own = slice(below, below + tile)
            buf[slot, at, own, :] = buf[slot, at, own, :] * keep
        return carry

    lax.fori_loop(0, tile, one, 0)


def col_kernel(
    slot_hbm, table_hbm, dft_hbm, res_hbm, spec_ref, out_ref, g_ref, meta_ref,
    buf, dft_ref, slot_ref, table_ref, one_ref, two_ref, acc_ref, sems,
):
    small = [
        pltpu.make_async_copy(src, dst, sems.at[SLOTS + n])
        for n, (src, dst) in enumerate(((slot_hbm, slot_ref), (table_hbm, table_ref), (dft_hbm, dft_ref)))
    ]
    for copy in small:
        copy.start()
    for n in range(3):
        chunk_copy(res_hbm, buf, sems, n, n).start()
    acc_ref[...] = jnp.zeros_like(acc_ref)
    for copy in small:
        copy.wait()
    for s in range(SLOTS):
        tile = slot_ref[s]
        safe = jnp.maximum(tile, 0)
        meta_ref[s] = table_ref[0, safe]
        meta_ref[SLOTS + s] = table_ref[1, safe]
        meta_ref[2 * SLOTS + s] = jnp.where(tile >= 0, 1, 0)

    for s in range(SLOTS):
        one, two = spec_pair(spec_ref, meta_ref[s] // 16, meta_ref[2 * SLOTS + s])
        one_ref[s * BS : (s + 1) * BS, :] = one
        two_ref[s * BS : (s + 1) * BS, :] = two

    def part(h, carry):
        s = h // PER
        first = (h - s * PER) * CHUNK
        slot = h
        p, q = meta_ref[s], meta_ref[SLOTS + s]

        chunk_copy(res_hbm, buf, sems, h, slot).wait()

        for c in range(PER):

            @pl.when((p == q) & (first == c * CHUNK))
            def _():
                mask_chunk(buf, slot, c * CHUNK)

        half = q // 16
        t1 = jnp.zeros((BS, 2 * F), jnp.float32)
        t2 = jnp.zeros((BS, 2 * F), jnp.float32)
        for u in range(0, CHUNK, 2):
            lhs = jnp.concatenate([buf[slot, u], buf[slot, u + 1]], axis=1)
            g = jnp.dot(lhs, dft_ref[...], preferred_element_type=jnp.float32)
            for k in range(2):
                gk = g[:, k * L : (k + 1) * L]
                g_ref[h * CHUNK + u + k] = gk
                t1 = t1 + gk * one_ref[pl.ds(h * CHUNK + u + k, 1), :]
                t2 = t2 + gk * two_ref[pl.ds(h * CHUNK + u + k, 1), :]
        acc_ref[half, 0] += t1
        acc_ref[half, 1] += t2
        return carry

    lax.fori_loop(0, PARTS, part, 0)
    lane = lax.broadcasted_iota(jnp.int32, (BS, 2 * F), 1)
    for half in range(2):
        t1, t2 = acc_ref[half, 0], acc_ref[half, 1]
        gain = jnp.where(lane < F, t1 + pltpu.roll(t1, F, axis=1), pltpu.roll(t2, F, axis=1) - t2)
        out_ref[:, half * 8 : (half + 1) * 8, :] = gain.reshape(16, BS // 16, 2 * F).astype(out_ref.dtype)


def row_kernel(meta_ref, spec_ref, g_ref, out_ref, one_ref, two_ref, part1, part2):
    out_ref[...] = jnp.zeros_like(out_ref)

    def slot(s, carry):
        p, q, filled = meta_ref[s], meta_ref[SLOTS + s], meta_ref[2 * SLOTS + s]
        one, two = spec_pair(spec_ref, q // 16, filled)
        one_ref[...] = one
        two_ref[...] = two

        def step(n, carry):
            for u in range(ROW_UNROLL):
                i = n * ROW_UNROLL + u
                g = g_ref[s * BS + i]
                at = pl.multiple_of(i * 8, 8)
                for ref, part in ((one_ref, part1), (two_ref, part2)):
                    prod = (g * ref[...]).reshape(BS // 8, 8, 2 * F)
                    part[pl.ds(at, 8), :] = jnp.sum(prod, axis=0)
            return carry

        lax.fori_loop(0, BS // ROW_UNROLL, step, 0)
        t1 = jnp.zeros((BS, 2 * F), jnp.float32)
        t2 = jnp.zeros((BS, 2 * F), jnp.float32)
        for k in range(8):
            t1 = t1 + part1[pl.ds(k, BS, stride=8), :]
            t2 = t2 + part2[pl.ds(k, BS, stride=8), :]
        lane = lax.broadcasted_iota(jnp.int32, (BS, 2 * F), 1)
        gain = jnp.where(lane < F, t1 - pltpu.roll(t1, F, axis=1), pltpu.roll(t2, F, axis=1) + t2)
        add_gain(out_ref, gain, p // 16)
        return carry

    lax.fori_loop(0, SLOTS, slot, 0)


def f32(*shape):
    return pltpu.VMEM(shape, jnp.float32)


VM = pl.BlockSpec(memory_space=pltpu.VMEM)
SM = pl.BlockSpec(memory_space=pltpu.SMEM)


def cost(flops, moved):
    return pl.CostEstimate(flops=flops, bytes_accessed=moved, transcendentals=0)


def gain_col(slot_tile, table, dft, residual, spec):
    far = pl.BlockSpec(memory_space=pl.ANY)
    held = [pltpu.with_memory_space_constraint(x, pltpu.HBM) for x in (slot_tile, table, dft, residual)]
    return pl.pallas_call(
        col_kernel,
        name="col_gain",
        out_shape=(
            jax.ShapeDtypeStruct((16, 16, 2 * F), jnp.bfloat16),
            jax.ShapeDtypeStruct((SLOTS * BS, BS, 2 * F), jnp.float32),
            jax.ShapeDtypeStruct((3 * SLOTS,), jnp.int32),
        ),
        in_specs=[far, far, far, far, VM],
        out_specs=(VM, VM, SM),
        scratch_shapes=[
            pltpu.VMEM((SLOTS, CHUNK, BS, L), jnp.bfloat16),
            pltpu.VMEM((2 * L, 4 * F), jnp.bfloat16),
            pltpu.SMEM((SLOTS,), jnp.int32),
            pltpu.SMEM(table.shape, jnp.int32),
            f32(SLOTS * BS, 2 * F),
            f32(SLOTS * BS, 2 * F),
            f32(2, 2, BS, 2 * F),
            pltpu.SemaphoreType.DMA((SLOTS + 3,)),
        ],
        compiler_params=pltpu.CompilerParams(vmem_limit_bytes=VMEM_COL),
        cost_estimate=cost(SLOTS * BS * BS * L * 2 * F * 4, residual.size * 2),
    )(*held, spec)


def gain_row(meta, spec, g):
    return pl.pallas_call(
        row_kernel,
        name="row_gain",
        out_shape=jax.ShapeDtypeStruct((16, 16, 2 * F), jnp.float32),
        in_specs=[SM, VM, VM],
        out_specs=VM,
        scratch_shapes=[f32(BS, 2 * F), f32(BS, 2 * F), f32(BS * 8, 2 * F), f32(BS * 8, 2 * F)],
        compiler_params=pltpu.CompilerParams(vmem_limit_bytes=VMEM_ROW),
        cost_estimate=cost(g.size * 4, g.size * 4),
    )(meta, spec, g)


def hops(a, b, k):
    def ring(u, v, n):
        return min((u - v) % n, (v - u) % n)

    z = ring(a // 4 * 2 + b // 8, b // 4 * 2 + k // 8, 8)
    return z + ring(a % 4, b % 4, 4) + ring(b // 2 % 4, k // 2 % 4, 4)


def assign(cost):
    n = len(cost)
    u, v, row, way = [0] * (n + 1), [0] * (n + 1), [0] * (n + 1), [0] * (n + 1)
    for i in range(1, n + 1):
        row[0], at = i, 0
        least, used = [math.inf] * (n + 1), [False] * (n + 1)
        while row[at]:
            used[at] = True
            delta, nxt = math.inf, 0
            for j in range(1, n + 1):
                if not used[j]:
                    c = cost[row[at] - 1][j - 1] - u[row[at]] - v[j]
                    if c < least[j]:
                        least[j], way[j] = c, at
                    if least[j] < delta:
                        delta, nxt = least[j], j
            for j in range(n + 1):
                if used[j]:
                    u[row[j]] += delta
                    v[j] -= delta
                else:
                    least[j] -= delta
            at = nxt
        while at:
            row[at] = row[way[at]]
            at = way[at]
    return {row[j] - 1: j - 1 for j in range(1, n + 1)}


def partners():
    pairs = []
    for b in range(16):
        chosen = assign([[6 ** hops(a, b, k) for k in range(16)] for a in range(16)])
        pairs += [(a * 16 + b, b * 16 + chosen[a]) for a in range(16)]
    return pairs


def on_device(spectra, residual, slot_tile, tile_blocks):
    table = tile_blocks.T
    dft = jnp.asarray(dft_pair())
    pairs = partners()
    spread = jnp.broadcast_to(spectra[None], (16, 16, 2 * F))
    row_spec = lax.all_to_all(spread, "col", 0, 0)
    col_spec = lax.ppermute(row_spec, ("row", "col"), [(v, u) for u, v in pairs])
    col_gain, g, meta = gain_col(slot_tile, table, dft, residual.reshape(SLOTS * BS, BS, L), row_spec)
    moved = lax.ppermute(col_gain, ("row", "col"), pairs)
    row_gain = gain_row(meta, col_spec, g)
    total = (row_gain + moved.astype(jnp.float32)).astype(jnp.bfloat16)
    pieces = lax.all_to_all(total, "col", 0, 0)
    return jnp.sum(pieces.astype(jnp.float32), axis=0)


def solution(mesh):
    return jax.shard_map(
        on_device,
        mesh=mesh,
        in_specs=(
            P(("row", "col"), None),
            P(("row", "col"), None, None, None),
            P(("row", "col")),
            P(),
        ),
        out_specs=P(("row", "col"), None),
        check_vma=False,
    )
```

```python
import functools
import math

import jax
import jax.numpy as jnp
import ml_dtypes
import numpy as np
from jax import lax
from jax.experimental import pallas as pl
from jax.experimental.pallas import tpu as pltpu
from jax.sharding import PartitionSpec as P

F = 64
L = 128
BS = 128
SLOTS = 3
NB = 32
CHUNK = 64
PARTS = SLOTS * BS // CHUNK
PER = BS // CHUNK
ROW_UNROLL = 64
VMEM_COL = 14 << 20
VMEM_ROW = 8 << 20


def dft_pair():
    lag = np.arange(L, dtype=np.int64) - L // 2
    freq = np.arange(F, dtype=np.int64)
    steps = (lag[:, None] * freq[None, :]) % L
    angles = steps.astype(np.float32) * np.float32(2.0 * math.pi / L)
    table = np.concatenate([np.cos(angles) / L, -np.sin(angles) / L], axis=1)
    zero = np.zeros((L, 2 * F))
    return np.block([[table, zero], [zero, table]]).astype(ml_dtypes.bfloat16)


def spec_pair(spec_ref, upper, filled):
    both = spec_ref[...].astype(jnp.float32)
    block = jnp.where(upper == 1, both[:, BS // 16 :, :], both[:, : BS // 16, :])
    block = block.reshape(BS, 2 * F) * filled.astype(jnp.float32)
    return block, pltpu.roll(block, F, axis=1)


def add_gain(ref, gain, half):
    gain = gain.reshape(16, BS // 16, 2 * F)
    for h in range(2):
        rows = pl.ds(h * 8, 8)

        @pl.when(half == h)
        def _():
            ref[:, rows, :] = ref[:, rows, :] + gain


def chunk_copy(res_hbm, buf, sems, h, slot):
    return pltpu.make_async_copy(res_hbm.at[pl.ds(h * CHUNK, CHUNK)], buf.at[slot], sems.at[slot])


def mask_chunk(buf, slot, first):
    tile = 16

    def one(r, carry):
        rows = lax.broadcasted_iota(jnp.int32, (tile, L), 0)
        keep = jnp.where(rows > r, 1.0, 0.0).astype(jnp.bfloat16)
        for m in range(CHUNK // tile):
            below = first + m * tile
            at = m * tile + r
            if below:
                buf[slot, at, :below, :] = jnp.zeros((below, L), jnp.bfloat16)
            own = slice(below, below + tile)
            buf[slot, at, own, :] = buf[slot, at, own, :] * keep
        return carry

    lax.fori_loop(0, tile, one, 0)


def col_kernel(
    slot_hbm, table_hbm, dft_hbm, res_hbm, spec_ref, out_ref, g_ref, meta_ref,
    buf, dft_ref, slot_ref, table_ref, one_ref, two_ref, acc_ref, sems,
):
    small = [
        pltpu.make_async_copy(src, dst, sems.at[PARTS + n])
        for n, (src, dst) in enumerate(((slot_hbm, slot_ref), (table_hbm, table_ref), (dft_hbm, dft_ref)))
    ]
    for copy in small:
        copy.start()
    for n in range(PARTS):
        chunk_copy(res_hbm, buf, sems, n, n).start()
    acc_ref[...] = jnp.zeros_like(acc_ref)
    for copy in small:
        copy.wait()
    for s in range(SLOTS):
        tile = slot_ref[s]
        safe = jnp.maximum(tile, 0)
        meta_ref[s] = table_ref[0, safe]
        meta_ref[SLOTS + s] = table_ref[1, safe]
        meta_ref[2 * SLOTS + s] = jnp.where(tile >= 0, 1, 0)

    for s in range(SLOTS):
        one, two = spec_pair(spec_ref, meta_ref[s] // 16, meta_ref[2 * SLOTS + s])
        one_ref[s * BS : (s + 1) * BS, :] = one
        two_ref[s * BS : (s + 1) * BS, :] = two

    def part(h, carry):
        s = h // PER
        first = (h - s * PER) * CHUNK
        slot = h
        p, q = meta_ref[s], meta_ref[SLOTS + s]

        chunk_copy(res_hbm, buf, sems, h, slot).wait()

        for c in range(PER):

            @pl.when((p == q) & (first == c * CHUNK))
            def _():
                mask_chunk(buf, slot, c * CHUNK)

        half = q // 16
        t1 = jnp.zeros((BS, 2 * F), jnp.float32)
        t2 = jnp.zeros((BS, 2 * F), jnp.float32)
        for u in range(0, CHUNK, 2):
            lhs = jnp.concatenate([buf[slot, u], buf[slot, u + 1]], axis=1)
            g = jnp.dot(lhs, dft_ref[...], preferred_element_type=jnp.float32)
            for k in range(2):
                gk = g[:, k * L : (k + 1) * L]
                g_ref[h * CHUNK + u + k] = gk
                t1 = t1 + gk * one_ref[pl.ds(h * CHUNK + u + k, 1), :]
                t2 = t2 + gk * two_ref[pl.ds(h * CHUNK + u + k, 1), :]
        acc_ref[half, 0] += t1
        acc_ref[half, 1] += t2
        return carry

    lax.fori_loop(0, PARTS, part, 0)
    lane = lax.broadcasted_iota(jnp.int32, (BS, 2 * F), 1)
    for half in range(2):
        t1, t2 = acc_ref[half, 0], acc_ref[half, 1]
        gain = jnp.where(lane < F, t1 + pltpu.roll(t1, F, axis=1), pltpu.roll(t2, F, axis=1) - t2)
        out_ref[:, half * 8 : (half + 1) * 8, :] = gain.reshape(16, BS // 16, 2 * F).astype(out_ref.dtype)


def row_kernel(meta_ref, spec_ref, g_ref, out_ref, one_ref, two_ref, part1, part2):
    out_ref[...] = jnp.zeros_like(out_ref)

    def slot(s, carry):
        p, q, filled = meta_ref[s], meta_ref[SLOTS + s], meta_ref[2 * SLOTS + s]
        one, two = spec_pair(spec_ref, q // 16, filled)
        one_ref[...] = one
        two_ref[...] = two

        def step(n, carry):
            for u in range(ROW_UNROLL):
                i = n * ROW_UNROLL + u
                g = g_ref[s * BS + i]
                at = pl.multiple_of(i * 8, 8)
                for ref, part in ((one_ref, part1), (two_ref, part2)):
                    prod = (g * ref[...]).reshape(BS // 8, 8, 2 * F)
                    part[pl.ds(at, 8), :] = jnp.sum(prod, axis=0)
            return carry

        lax.fori_loop(0, BS // ROW_UNROLL, step, 0)
        t1 = jnp.zeros((BS, 2 * F), jnp.float32)
        t2 = jnp.zeros((BS, 2 * F), jnp.float32)
        for k in range(8):
            t1 = t1 + part1[pl.ds(k, BS, stride=8), :]
            t2 = t2 + part2[pl.ds(k, BS, stride=8), :]
        lane = lax.broadcasted_iota(jnp.int32, (BS, 2 * F), 1)
        gain = jnp.where(lane < F, t1 - pltpu.roll(t1, F, axis=1), pltpu.roll(t2, F, axis=1) + t2)
        add_gain(out_ref, gain, p // 16)
        return carry

    lax.fori_loop(0, SLOTS, slot, 0)


def f32(*shape):
    return pltpu.VMEM(shape, jnp.float32)


VM = pl.BlockSpec(memory_space=pltpu.VMEM)
SM = pl.BlockSpec(memory_space=pltpu.SMEM)


def cost(flops, moved):
    return pl.CostEstimate(flops=flops, bytes_accessed=moved, transcendentals=0)


def gain_col(slot_tile, table, dft, residual, spec):
    far = pl.BlockSpec(memory_space=pl.ANY)
    held = [pltpu.with_memory_space_constraint(x, pltpu.HBM) for x in (slot_tile, table, dft, residual)]
    return pl.pallas_call(
        col_kernel,
        name="col_gain",
        out_shape=(
            jax.ShapeDtypeStruct((16, 16, 2 * F), jnp.bfloat16),
            jax.ShapeDtypeStruct((SLOTS * BS, BS, 2 * F), jnp.float32),
            jax.ShapeDtypeStruct((3 * SLOTS,), jnp.int32),
        ),
        in_specs=[far, far, far, far, VM],
        out_specs=(VM, VM, SM),
        scratch_shapes=[
            pltpu.VMEM((PARTS, CHUNK, BS, L), jnp.bfloat16),
            pltpu.VMEM((2 * L, 4 * F), jnp.bfloat16),
            pltpu.SMEM((SLOTS,), jnp.int32),
            pltpu.SMEM(table.shape, jnp.int32),
            f32(SLOTS * BS, 2 * F),
            f32(SLOTS * BS, 2 * F),
            f32(2, 2, BS, 2 * F),
            pltpu.SemaphoreType.DMA((PARTS + 3,)),
        ],
        compiler_params=pltpu.CompilerParams(vmem_limit_bytes=VMEM_COL),
        cost_estimate=cost(SLOTS * BS * BS * L * 2 * F * 4, residual.size * 2),
    )(*held, spec)


def gain_row(meta, spec, g):
    return pl.pallas_call(
        row_kernel,
        name="row_gain",
        out_shape=jax.ShapeDtypeStruct((16, 16, 2 * F), jnp.float32),
        in_specs=[SM, VM, VM],
        out_specs=VM,
        scratch_shapes=[f32(BS, 2 * F), f32(BS, 2 * F), f32(BS * 8, 2 * F), f32(BS * 8, 2 * F)],
        compiler_params=pltpu.CompilerParams(vmem_limit_bytes=VMEM_ROW),
        cost_estimate=cost(g.size * 4, g.size * 4),
    )(meta, spec, g)


def hops(a, b, k):
    def ring(u, v, n):
        return min((u - v) % n, (v - u) % n)

    z = ring(a // 4 * 2 + b // 8, b // 4 * 2 + k // 8, 8)
    return z + ring(a % 4, b % 4, 4) + ring(b // 2 % 4, k // 2 % 4, 4)


def assign(cost):
    n = len(cost)
    u, v, row, way = [0] * (n + 1), [0] * (n + 1), [0] * (n + 1), [0] * (n + 1)
    for i in range(1, n + 1):
        row[0], at = i, 0
        least, used = [math.inf] * (n + 1), [False] * (n + 1)
        while row[at]:
            used[at] = True
            delta, nxt = math.inf, 0
            for j in range(1, n + 1):
                if not used[j]:
                    c = cost[row[at] - 1][j - 1] - u[row[at]] - v[j]
                    if c < least[j]:
                        least[j], way[j] = c, at
                    if least[j] < delta:
                        delta, nxt = least[j], j
            for j in range(n + 1):
                if used[j]:
                    u[row[j]] += delta
                    v[j] -= delta
                else:
                    least[j] -= delta
            at = nxt
        while at:
            row[at] = row[way[at]]
            at = way[at]
    return {row[j] - 1: j - 1 for j in range(1, n + 1)}


def partners():
    pairs = []
    for b in range(16):
        chosen = assign([[6 ** hops(a, b, k) for k in range(16)] for a in range(16)])
        pairs += [(a * 16 + b, b * 16 + chosen[a]) for a in range(16)]
    return pairs


def on_device(spectra, residual, slot_tile, tile_blocks):
    table = tile_blocks.T
    dft = jnp.asarray(dft_pair())
    pairs = partners()
    spread = jnp.broadcast_to(spectra[None], (16, 16, 2 * F))
    row_spec = lax.all_to_all(spread, "col", 0, 0)
    col_spec = lax.ppermute(row_spec, ("row", "col"), [(v, u) for u, v in pairs])
    col_gain, g, meta = gain_col(slot_tile, table, dft, residual.reshape(SLOTS * BS, BS, L), row_spec)
    moved = lax.ppermute(col_gain, ("row", "col"), pairs)
    row_gain = gain_row(meta, col_spec, g)
    total = (row_gain + moved.astype(jnp.float32)).astype(jnp.bfloat16)
    pieces = lax.all_to_all(total, "col", 0, 0)
    return jnp.sum(pieces.astype(jnp.float32), axis=0)


def solution(mesh):
    return jax.shard_map(
        on_device,
        mesh=mesh,
        in_specs=(
            P(("row", "col"), None),
            P(("row", "col"), None, None, None),
            P(("row", "col")),
            P(),
        ),
        out_specs=P(("row", "col"), None),
        check_vma=False,
    )
```
